32 devices in a mesh: sec: 2 (over core), blk: 8 (over z, x), ch: 2 (over y).
Axes of the slice: x: 2, y: 2, z: 4, core: 2. Of those that a mesh axis runs over, the one named last changes fastest.
Arguments:
- voltages: bfloat16 [123, 4096, 2048], P(None, 'blk', ('sec', 'ch')), may hold values from -6 to 6
Outputs:
- visibilities: bfloat16 [16, 2, 4096, 4096], P(('sec', 'ch'), None, 'blk')
The draws below stay inside these ranges and needn't reach their ends.
All inputs are finite; a program needn't handle non-finite values.
Results may differ from the reference program's by a relative error of at most 0.0082.
Values may be sent and summed in bfloat16 or wider, within the bound.
A program may use at most 384 MiB of HBM per device.

```python
import math
import jax
import jax.numpy as jnp
from jax import lax

STREAMS = 4096
FFT = 2048
TAPS = 4
TIME = 120
NCHAN = 1024
CHAN = 16
FRAMES = 123
PANEL = 512
N_BLK = 8


def steps_of(key, extent, shards, least, high):
    def one(dim, blocks):
        draws = jax.random.uniform(jax.random.fold_in(jax.random.fold_in(key, 6), dim), (blocks,), jnp.float32, least / len(shards), high / len(shards))
        return jnp.repeat(jnp.exp(draws), extent[dim] // blocks).reshape((-1,) + (1,) * (len(extent) - dim - 1))

    factor_of = one(*shards[0])
    for cut in shards[1:]:
        factor_of = factor_of * one(*cut)
    return factor_of


def bell_draw(rng, dims, width, most, shards=(), kind=jnp.bfloat16):
    entries = jax.random.normal(rng, dims, jnp.float32) * width
    if len(shards) > 0:
        entries = steps_of(rng, dims, shards, -0.22, 0.18) * entries
    return jnp.clip(entries, min=-most, max=most).astype(kind)


def setup_inputs(seed: int = 0) -> dict:
    seeds = jax.random.split(jax.random.key(seed), 2)
    return {
        "voltages": bell_draw(seeds[0], (FRAMES, STREAMS, FFT), 1.0, 6.0, ((1, 8), (2, 4))),
    }


def make_window(tap_count, frame_len):
    position = jnp.arange(tap_count * frame_len, dtype=jnp.float32)
    offset = (position - tap_count * frame_len / 2 + 0.5) / frame_len
    taper = 0.5 - 0.5 * jnp.cos(2.0 * jnp.pi * (position + 0.5) / (tap_count * frame_len))
    profile = jnp.sinc(offset) * taper
    profile = profile * jnp.sqrt(frame_len / jnp.sum(profile * profile))
    return profile.reshape(tap_count, frame_len)

def dft_table(frame_len, chan_count, bank_size):
    spacing = bank_size // chan_count
    chosen = jnp.arange(chan_count, dtype=jnp.int32) * spacing + spacing // 2
    phases = jnp.arange(frame_len, dtype=jnp.int32)[:, None] * chosen[None, :] % frame_len
    angles = 2.0 * jnp.pi / frame_len * phases.astype(jnp.float32)
    factor = 1.0 / math.sqrt(frame_len)
    weights = jnp.stack([jnp.cos(angles) * factor, -jnp.sin(angles) * factor], axis=-1)
    return weights.reshape(frame_len, chan_count * 2).astype(jnp.bfloat16)

def reference(voltages):
    window = make_window(TAPS, FFT)
    weights = dft_table(FFT, CHAN, NCHAN)

    def channelise(group_index):
        inputs_block = lax.dynamic_slice_in_dim(voltages, group_index * PANEL, PANEL, 1)
        summed = jnp.zeros((TIME, PANEL, FFT), jnp.float32)
        for tap_index in range(TAPS):
            summed = summed + window[tap_index] * inputs_block[tap_index:tap_index + TIME].astype(jnp.float32)
        filtered = summed.astype(jnp.bfloat16)
        spectrum = jnp.dot(filtered.reshape(TIME * PANEL, FFT), weights, preferred_element_type=jnp.float32)
        return spectrum.astype(jnp.bfloat16).reshape(TIME, PANEL, CHAN, 2)
    pieces = lax.map(channelise, jnp.arange(N_BLK, dtype=jnp.int32))
    spectra = pieces.transpose(3, 4, 1, 0, 2).reshape(CHAN, 2, TIME, STREAMS)

    def correlate(chan_spectra):
        real_part = chan_spectra[0]
        imag_part = chan_spectra[1]
        real_sum = jnp.dot(real_part.T, real_part, preferred_element_type=jnp.float32) + jnp.dot(imag_part.T, imag_part, preferred_element_type=jnp.float32)
        imag_sum = jnp.dot(imag_part.T, real_part, preferred_element_type=jnp.float32) - jnp.dot(real_part.T, imag_part, preferred_element_type=jnp.float32)
        return (jnp.stack([real_sum, imag_sum]) / TIME).astype(jnp.bfloat16)
    return lax.map(correlate, spectra)
```

```python
import functools

import jax
import jax.numpy as jnp
import ml_dtypes
import numpy as np
from jax import lax
from jax.experimental import pallas as pl
from jax.experimental.pallas import tpu as pltpu
from jax.sharding import PartitionSpec as P

FFT = 2048
NCHAN = 1024
TAPS = 4
CH_GRP = 4
LANES = 128
PART_STEPS = 40
LOADS = 4
LAG = 2
MESH = pl.DeviceIdType.MESH


def make_weights(groups):
    chan_total = CH_GRP * groups
    position = np.arange(TAPS * FFT, dtype=np.float64)
    taper = 0.5 - 0.5 * np.cos(2.0 * np.pi * (position + 0.5) / (TAPS * FFT))
    profile = np.sinc((position - TAPS * FFT / 2 + 0.5) / FFT) * taper
    profile = profile * np.sqrt(FFT / np.sum(profile * profile))
    window = profile.reshape(TAPS, FFT).astype(np.float32)
    spacing = NCHAN // chan_total
    row = np.arange(2 * chan_total)
    chosen = row // 2 * spacing + spacing // 2
    angles = 2.0 * np.pi * (chosen[:, None] * np.arange(FFT)[None, :] % FFT) / FFT
    wave = np.where(row[:, None] % 2 == 0, np.cos(angles), -np.sin(angles)) / np.sqrt(FFT)
    table = wave.astype(ml_dtypes.bfloat16).astype(np.float32)
    weights = (window[:, None, :] * table[None]).reshape(TAPS * 2 * chan_total, groups, FFT // groups)
    return np.ascontiguousarray(weights.transpose(1, 0, 2)).astype(ml_dtypes.bfloat16)


def spread_kernel(n, steps, volts_ref, table_ref, all_ref, own_ref, weights, volts, head, products, spectra, terms,
                  got_core, half, got_chip, weights_sem, volts_sems, head_sems, core_sems, chip_sems, ring_send,
                  ring_recv, local_sems):
    sec, ch, blk = lax.axis_index("sec"), lax.axis_index("ch"), lax.axis_index("blk")
    other_sec, other_ch = 1 - sec, 1 - ch
    pieces, group = own_ref.shape[0], own_ref.shape[1]
    hops = n // 2
    part_len = products.shape[0] - (TAPS - 1)
    parts = steps // part_len
    rows = weights.shape[0] // TAPS
    slots = volts.shape[0]

    def block_at(place):
        place = lax.rem(place + 2 * n, n)
        return 2 * place + place // (n // 2) * (2 * n - 1 - 4 * place)

    place = blk // 2 + lax.rem(blk, 2) * (n - 1 - 2 * (blk // 2))
    sides = (block_at(place + 1), block_at(place - 1))

    def weights_copy():
        return pltpu.make_async_copy(table_ref.at[sec * lax.axis_size("ch") + ch], weights, weights_sem)

    def volts_copy(k, load):
        slot = lax.rem(k, slots)
        count = part_len // LOADS
        first = lax.rem(k, parts) * part_len + TAPS - 1 + load * count
        return pltpu.make_async_copy(
            volts_ref.at[pl.ds(first, count), pl.ds(k // parts * LANES, LANES)],
            volts.at[slot, pl.ds(load * count, count)],
            volts_sems.at[slot, load],
        )

    def head_copy(q):
        slot = lax.rem(q, 2)
        return pltpu.make_async_copy(
            volts_ref.at[pl.ds(0, TAPS - 1), pl.ds(q * LANES, LANES)], head.at[slot], head_sems.at[slot]
        )

    def load_piece(k):
        @pl.when(lax.rem(k, parts) == 0)
        def _():
            head_copy(k // parts).start()

        for load in range(LOADS):
            volts_copy(k, load).start()

    def filtered(samples):
        return lax.dot_general(
            weights[...], samples, (((1,), (1,)), ((), ())), preferred_element_type=jnp.float32
        )

    def produce(k):
        part, slot = lax.rem(k, parts), lax.rem(k, slots)

        @pl.when(part == 0)
        def _():
            head_copy(k // parts).wait()
            for frame in range(TAPS - 1):
                products[frame] = filtered(head[lax.rem(k // parts, 2), frame])

        @pl.when(part > 0)
        def _():
            for frame in range(TAPS - 1):
                products[frame] = products[part_len + frame]

        count = part_len // LOADS
        for load in range(LOADS):
            volts_copy(k, load).wait()
            for frame in range(load * count, (load + 1) * count):
                products[TAPS - 1 + frame] = filtered(volts[slot, frame])

        def add_taps(step, carry):
            total = products[step, 0:rows]
            for tap in range(1, TAPS):
                total = total + products[step + tap, tap * rows : (tap + 1) * rows]
            spectra[pl.ds(step, rows, stride=part_len), :] = total
            return carry

        lax.fori_loop(0, part_len, add_taps, 0)
        terms[k] = spectra[...].reshape(terms.shape[1:]).astype(jnp.bfloat16)

    def core_copy(k):
        return pltpu.make_async_remote_copy(
            src_ref=terms.at[k, pl.ds(other_sec * 2 * group, 2 * group)],
            dst_ref=got_core.at[k],
            send_sem=core_sems.at[0, k],
            recv_sem=core_sems.at[1, k],
            device_id={"sec": other_sec},
            device_id_type=MESH,
        )

    def chip_copy(k):
        return pltpu.make_async_remote_copy(
            src_ref=half.at[k],
            dst_ref=got_chip.at[k],
            send_sem=chip_sems.at[0, k],
            recv_sem=chip_sems.at[1, k],
            device_id={"ch": other_ch},
            device_id_type=MESH,
        )

    def ring_copy(k, side, hop):
        origin = block_at(place - (hop - 1) * (1 - 2 * side))
        source = own_ref.at[k] if hop == 1 else all_ref.at[origin, k]
        target = all_ref.at[origin, k]
        if hop == hops:
            piece = pl.ds(side * (group // 2), group // 2)
            source, target = source.at[piece], target.at[piece]
        return pltpu.make_async_remote_copy(
            src_ref=source,
            dst_ref=target,
            send_sem=ring_send.at[side, hop - 1, k],
            recv_sem=ring_recv.at[side, hop - 1, k],
            device_id={"blk": sides[side]},
            device_id_type=MESH,
        )

    def local_copy(k):
        return pltpu.make_async_copy(own_ref.at[k], all_ref.at[blk, k], local_sems.at[k])

    def pair_sum(k, start):
        mine = terms[k, pl.ds(sec * 2 * group + start, group)].astype(jnp.float32)
        return mine + got_core[k, pl.ds(start, group)].astype(jnp.float32)

    def over_cores(k):
        core_copy(k).wait_recv()
        half[k] = pair_sum(k, other_ch * group).astype(jnp.bfloat16)
        chip_copy(k).start()

    def over_chips(k):
        total = pair_sum(k, ch * group)
        chip_copy(k).wait_recv()
        own_ref[k] = (total + got_chip[k].astype(jnp.float32)).astype(jnp.bfloat16)
        for side in range(2):
            ring_copy(k, side, 1).start()
        local_copy(k).start()

    def forward(k, hop):
        for side in range(2):
            ring_copy(k, side, hop).wait_recv()
            ring_copy(k, side, hop + 1).start()

    def when_piece(k, act, *values):
        @pl.when((k >= 0) & (k < pieces))
        def _():
            act(k, *values)

    weights_copy().start()
    for k in range(slots - 1):
        load_piece(k)
    barrier = pltpu.get_barrier_semaphore()
    partners = ({"sec": other_sec}, {"ch": other_ch}, {"blk": sides[0]}, {"blk": sides[1]})
    for partner in partners:
        pl.semaphore_signal(barrier, inc=1, device_id=partner, device_id_type=MESH)
    weights_copy().wait()

    def one_step(step, carry):
        @pl.when(step < pieces)
        def _():
            @pl.when(step + slots - 1 < pieces)
            def _():
                load_piece(step + slots - 1)

            produce(step)
            @pl.when(step == 0)
            def _():
                pl.semaphore_wait(barrier, len(partners))

            core_copy(step).start()

        for hop in range(hops - 1, 0, -1):
            when_piece(step - 2 - LAG * hop, forward, hop)
        when_piece(step - 2, over_chips)
        when_piece(step - 1, over_cores)
        return carry

    lax.fori_loop(0, pieces + 2 + LAG * (hops - 1), one_step, 0)

    def finish(k, carry):
        core_copy(k).wait_send()
        chip_copy(k).wait_send()
        local_copy(k).wait()
        for side in range(2):
            ring_copy(k, side, hops).wait_recv()
            for hop in range(1, hops + 1):
                ring_copy(k, side, hop).wait_send()
        return carry

    lax.fori_loop(0, pieces, finish, 0)


def spread(voltages, table):
    n = lax.axis_size("blk")
    frames, panel_len, span_len = voltages.shape
    steps = frames - TAPS + 1
    taps_rows = table.shape[1]
    rows = taps_rows // TAPS
    parts = steps // PART_STEPS
    pieces, depth = panel_len // LANES * parts, 2 * PART_STEPS
    group = rows // 2 // (lax.axis_size("sec") * lax.axis_size("ch"))
    piece = (pieces, group, depth, LANES)
    slots = 3
    return pl.pallas_call(
        functools.partial(spread_kernel, n, steps),
        in_specs=[pl.BlockSpec(memory_space=pl.ANY), pl.BlockSpec(memory_space=pl.ANY)],
        out_specs=[pl.BlockSpec(memory_space=pl.ANY), pl.BlockSpec(memory_space=pltpu.VMEM)],
        out_shape=[
            jax.ShapeDtypeStruct((n,) + piece, jnp.bfloat16),
            jax.ShapeDtypeStruct(piece, jnp.bfloat16),
        ],
        scratch_shapes=[
            pltpu.VMEM((taps_rows, span_len), jnp.bfloat16),
            pltpu.VMEM((slots, PART_STEPS, LANES, span_len), jnp.bfloat16),
            pltpu.VMEM((2, TAPS - 1, LANES, span_len), jnp.bfloat16),
            pltpu.VMEM((PART_STEPS + TAPS - 1, taps_rows, LANES), jnp.float32),
            pltpu.VMEM((rows * PART_STEPS, LANES), jnp.float32),
            pltpu.VMEM((pieces, rows // 2, depth, LANES), jnp.bfloat16),
            pltpu.VMEM((pieces, 2 * group, depth, LANES), jnp.bfloat16),
            pltpu.VMEM(piece, jnp.bfloat16),
            pltpu.VMEM(piece, jnp.bfloat16),
            pltpu.SemaphoreType.DMA,
            pltpu.SemaphoreType.DMA((slots, LOADS)),
            pltpu.SemaphoreType.DMA((2,)),
            pltpu.SemaphoreType.DMA((2, pieces)),
            pltpu.SemaphoreType.DMA((2, pieces)),
            pltpu.SemaphoreType.DMA((2, n // 2, pieces)),
            pltpu.SemaphoreType.DMA((2, n // 2, pieces)),
            pltpu.SemaphoreType.DMA((pieces,)),
        ],
        compiler_params=pltpu.CompilerParams(
            collective_id=0, has_side_effects=True, vmem_limit_bytes=56 * 1024 * 1024
        ),
    )(voltages, table)


def pair_kernel(parts, local_ref, remote_ref, out_ref, lhs):
    pieces, depth, lanes = local_ref.shape[0], local_ref.shape[2], local_ref.shape[3]
    chunks, half = pieces // parts, depth // 2
    panel_len = chunks * lanes
    steps = half * parts

    @pl.when(pl.program_id(1) == 0)
    def _():
        for q in range(chunks):
            straight, crossed = [], []
            for part in range(parts):
                values = local_ref[q * parts + part, 0].astype(jnp.float32)
                straight.append(values)
                crossed += [values[half:], -values[:half]]
            lhs[q * lanes : (q + 1) * lanes, :] = jnp.concatenate(straight, axis=0).T.astype(jnp.bfloat16)
            low = panel_len + q * lanes
            lhs[low : low + lanes, :] = jnp.concatenate(crossed, axis=0).T.astype(jnp.bfloat16)

    for place in range(remote_ref.shape[0]):
        remote = jnp.concatenate(
            [
                jnp.concatenate([remote_ref[place, q * parts + part, 0] for part in range(parts)], axis=0)
                for q in range(chunks)
            ],
            axis=1,
        )
        sums = jnp.dot(lhs[...], remote, preferred_element_type=jnp.float32)
        scaled = (sums * (1.0 / steps)).astype(jnp.bfloat16)
        span = slice(place * panel_len, (place + 1) * panel_len)
        out_ref[0, 0, :, span] = scaled[:panel_len]
        out_ref[0, 1, :, span] = scaled[panel_len:]


def correlate(local, gathered, parts):
    panels, pieces, chans, depth, lanes = gathered.shape
    panel_len = pieces // parts * lanes
    batch = 8 if panels % 8 == 0 else 1
    return pl.pallas_call(
        functools.partial(pair_kernel, parts),
        grid=(chans, panels // batch),
        in_specs=[
            pl.BlockSpec((pieces, 1, depth, lanes), lambda c, j: (0, c, 0, 0)),
            pl.BlockSpec((batch, pieces, 1, depth, lanes), lambda c, j: (j, 0, c, 0, 0)),
        ],
        out_specs=pl.BlockSpec((1, 2, panel_len, batch * panel_len), lambda c, j: (c, 0, 0, j)),
        out_shape=jax.ShapeDtypeStruct((chans, 2, panel_len, panels * panel_len), jnp.bfloat16),
        scratch_shapes=[pltpu.VMEM((2 * panel_len, depth * parts), jnp.bfloat16)],
        compiler_params=pltpu.CompilerParams(vmem_limit_bytes=56 * 1024 * 1024),
    )(local, gathered)


def body(voltages):
    groups = lax.axis_size("sec") * lax.axis_size("ch")
    parts = (voltages.shape[0] - TAPS + 1) // PART_STEPS
    gathered, own = spread(voltages, jnp.asarray(make_weights(groups)))
    return correlate(own, gathered, parts)


def solution(mesh):
    return jax.shard_map(
        body,
        mesh=mesh,
        in_specs=(P(None, "blk", ("sec", "ch")),),
        out_specs=P(("sec", "ch"), None, "blk", None),
        check_vma=False,
    )
```

```python
import functools

import jax
import jax.numpy as jnp
import ml_dtypes
import numpy as np
from jax import lax
from jax.experimental import pallas as pl
from jax.experimental.pallas import tpu as pltpu
from jax.sharding import PartitionSpec as P

FFT = 2048
NCHAN = 1024
TAPS = 4
CH_GRP = 4
LANES = 128
PART_STEPS = 40
LOADS = 4
LAG = 2
CHIP_LAG = 1
AHEAD = 6
SPREAD_VMEM = 40 * 1024 * 1024
PAIR_VMEM = 40 * 1024 * 1024
MESH = pl.DeviceIdType.MESH


def make_weights(groups):
    chan_total = CH_GRP * groups
    position = np.arange(TAPS * FFT, dtype=np.float64)
    taper = 0.5 - 0.5 * np.cos(2.0 * np.pi * (position + 0.5) / (TAPS * FFT))
    profile = np.sinc((position - TAPS * FFT / 2 + 0.5) / FFT) * taper
    profile = profile * np.sqrt(FFT / np.sum(profile * profile))
    window = profile.reshape(TAPS, FFT).astype(np.float32)
    spacing = NCHAN // chan_total
    row = np.arange(2 * chan_total)
    chosen = row // 2 * spacing + spacing // 2
    angles = 2.0 * np.pi * (chosen[:, None] * np.arange(FFT)[None, :] % FFT) / FFT
    wave = np.where(row[:, None] % 2 == 0, np.cos(angles), -np.sin(angles)) / np.sqrt(FFT)
    table = wave.astype(ml_dtypes.bfloat16).astype(np.float32)
    weights = (window[:, None, :] * table[None]).reshape(TAPS * 2 * chan_total, groups, FFT // groups)
    return np.ascontiguousarray(weights.transpose(1, 0, 2)).astype(ml_dtypes.bfloat16)


def block_at(place, n):
    place = lax.rem(place + 2 * n, n)
    return 2 * place + place // (n // 2) * (2 * n - 1 - 4 * place)


def place_of(blk, n):
    return blk // 2 + lax.rem(blk, 2) * (n - 1 - 2 * (blk // 2))


def spread_kernel(n, steps, volts_ref, table_ref, lhs_ref, own_ref, near_ref, low0, high0, low1, high1, weights, volts,
                  head, products, spectra, terms, got_core, half, got_chip, own, lhs, weights_sem, volts_sems, head_sems,
                  core_sems, chip_sems, near_send, near_recv, far_send, far_recv, own_sems, lhs_sems):
    sec, ch, blk = lax.axis_index("sec"), lax.axis_index("ch"), lax.axis_index("blk")
    other_sec, other_ch = 1 - sec, 1 - ch
    pieces, group = own.shape[0], own.shape[1]
    far_refs = ((low0, high0), (low1, high1))
    last = n // 2 - 1
    part_len = products.shape[0] - (TAPS - 1)
    parts = steps // part_len
    rows = weights.shape[0] // TAPS
    slots = volts.shape[0]
    place = place_of(blk, n)
    sides = (block_at(place + 1, n), block_at(place - 1, n))

    def weights_copy():
        return pltpu.make_async_copy(table_ref.at[sec * lax.axis_size("ch") + ch], weights, weights_sem)

    def volts_copy(load):
        slot = lax.rem(load, slots)
        count = volts.shape[1]
        k = load // LOADS
        first = lax.rem(k, parts) * part_len + TAPS - 1 + lax.rem(load, LOADS) * count
        return pltpu.make_async_copy(
            volts_ref.at[pl.ds(first, count), pl.ds(k // parts * LANES, LANES)], volts.at[slot], volts_sems.at[slot]
        )

    def head_copy(q):
        slot = lax.rem(q, 2)
        return pltpu.make_async_copy(
            volts_ref.at[pl.ds(0, TAPS - 1), pl.ds(q * LANES, LANES)], head.at[slot], head_sems.at[slot]
        )

    def filtered(samples):
        return lax.dot_general(
            weights[...], samples, (((1,), (1,)), ((), ())), preferred_element_type=jnp.float32
        )

    def produce(k):
        part = lax.rem(k, parts)

        @pl.when(part == 0)
        def _():
            q = k // parts
            head_copy(q).wait()

            @pl.when(q + 1 < pieces // parts)
            def _():
                head_copy(q + 1).start()

            for frame in range(TAPS - 1):
                products[frame] = filtered(head[lax.rem(q, 2), frame])

        @pl.when(part > 0)
        def _():
            for frame in range(TAPS - 1):
                products[frame] = products[part_len + frame]

        count = volts.shape[1]
        for index in range(LOADS):
            load = k * LOADS + index
            volts_copy(load).wait()

            @pl.when(load + AHEAD < pieces * LOADS)
            def _():
                volts_copy(load + AHEAD).start()

            slot = lax.rem(load, slots)
            for frame in range(count):
                products[TAPS - 1 + index * count + frame] = filtered(volts[slot, frame])

        def add_taps(step, carry):
            total = products[step, 0:rows]
            for tap in range(1, TAPS):
                total = total + products[step + tap, tap * rows : (tap + 1) * rows]
            spectra[pl.ds(step, rows, stride=part_len), :] = total
            return carry

        lax.fori_loop(0, part_len, add_taps, 0)
        terms[k] = spectra[...].reshape(terms.shape[1:]).astype(jnp.bfloat16)

    def core_copy(k):
        return pltpu.make_async_remote_copy(
            src_ref=terms.at[k, pl.ds(other_sec * 2 * group, 2 * group)],
            dst_ref=got_core.at[k],
            send_sem=core_sems.at[0, k],
            recv_sem=core_sems.at[1, k],
            device_id={"sec": other_sec},
            device_id_type=MESH,
        )

    def chip_copy(k):
        return pltpu.make_async_remote_copy(
            src_ref=half.at[k],
            dst_ref=got_chip.at[k],
            send_sem=chip_sems.at[0, k],
            recv_sem=chip_sems.at[1, k],
            device_id={"ch": other_ch},
            device_id_type=MESH,
        )

    def ring_copies(k, side, hop):
        source = own.at[k] if hop == 1 else near_ref.at[2 * (hop - 2) + side, k]
        if hop < last:
            moves = [(source, near_ref.at[2 * (hop - 1) + side, k], near_send.at[side, hop - 1, k],
                      near_recv.at[side, hop - 1, k])]
        else:
            moves = [
                (source.at[pl.ds(part * (group // 2), group // 2)], far_refs[side][part].at[k],
                 far_send.at[side, part, k], far_recv.at[side, part, k])
                for part in range(2)
            ]
        return [
            pltpu.make_async_remote_copy(
                src_ref=src,
                dst_ref=dst,
                send_sem=send,
                recv_sem=recv,
                device_id={"blk": sides[side]},
                device_id_type=MESH,
            )
            for src, dst, send, recv in moves
        ]

    def pair_sum(k, start):
        mine = terms[k, pl.ds(sec * 2 * group + start, group)].astype(jnp.float32)
        return mine + got_core[k, pl.ds(start, group)].astype(jnp.float32)

    def own_copy(k):
        return pltpu.make_async_copy(own.at[k], own_ref.at[k], own_sems.at[k])

    def lhs_copy(q):
        rows_of = pl.ds(q * LANES, LANES)
        return pltpu.make_async_copy(lhs.at[:, :, rows_of], lhs_ref.at[:, :, rows_of], lhs_sems.at[q])

    def turn(q):
        rows_of = pl.ds(pl.multiple_of(q * LANES, LANES), LANES)
        for c in range(group):
            straight, crossed = [], []
            for part in range(parts):
                values = own[q * parts + part, c].astype(jnp.float32)
                straight.append(values)
                crossed += [values[part_len:], -values[:part_len]]
            lhs[c, 0, rows_of, :] = jnp.concatenate(straight, axis=0).T.astype(jnp.bfloat16)
            lhs[c, 1, rows_of, :] = jnp.concatenate(crossed, axis=0).T.astype(jnp.bfloat16)
        lhs_copy(q).start()

    def over_cores(k):
        core_copy(k).wait_recv()
        half[k] = pair_sum(k, other_ch * group).astype(jnp.bfloat16)
        chip_copy(k).start()

    def over_chips(k):
        total = pair_sum(k, ch * group)
        chip_copy(k).wait_recv()
        own[k] = (total + got_chip[k].astype(jnp.float32)).astype(jnp.bfloat16)
        for side in range(2):
            for copy in ring_copies(k, side, 1):
                copy.start()
        own_copy(k).start()

        @pl.when(lax.rem(k, parts) == parts - 1)
        def _():
            turn(k // parts)

    def forward(k, hop):
        for side in range(2):
            for copy in ring_copies(k, side, hop):
                copy.wait_recv()
            for copy in ring_copies(k, side, hop + 1):
                copy.start()

    def when_piece(k, act, *values):
        @pl.when((k >= 0) & (k < pieces))
        def _():
            act(k, *values)

    weights_copy().start()
    head_copy(0).start()
    for load in range(AHEAD):
        volts_copy(load).start()
    barrier = pltpu.get_barrier_semaphore()
    partners = ({"sec": other_sec}, {"ch": other_ch}, {"blk": sides[0]}, {"blk": sides[1]})
    for partner in partners:
        pl.semaphore_signal(barrier, inc=1, device_id=partner, device_id_type=MESH)
    weights_copy().wait()

    def one_step(step, carry):
        @pl.when(step < pieces)
        def _():
            produce(step)

            @pl.when(step == 0)
            def _():
                pl.semaphore_wait(barrier, len(partners))

            core_copy(step).start()

        for hop in range(last - 1, 0, -1):
            when_piece(step - 1 - CHIP_LAG - LAG * hop, forward, hop)
        when_piece(step - 1 - CHIP_LAG, over_chips)
        when_piece(step - 1, over_cores)
        return carry

    lax.fori_loop(0, pieces + 1 + CHIP_LAG + LAG * (last - 1), one_step, 0)

    def finish(k, carry):
        core_copy(k).wait_send()
        chip_copy(k).wait_send()
        own_copy(k).wait()
        for side in range(2):
            for copy in ring_copies(k, side, last):
                copy.wait_recv()
            for hop in range(1, last + 1):
                for copy in ring_copies(k, side, hop):
                    copy.wait_send()
        return carry

    lax.fori_loop(0, pieces, finish, 0)
    for q in range(pieces // parts):
        lhs_copy(q).wait()


def spread(voltages, table):
    n = lax.axis_size("blk")
    frames, panel_len, span_len = voltages.shape
    steps = frames - TAPS + 1
    taps_rows = table.shape[1]
    rows = taps_rows // TAPS
    parts = steps // PART_STEPS
    pieces, depth = panel_len // LANES * parts, 2 * PART_STEPS
    group = rows // 2 // (lax.axis_size("sec") * lax.axis_size("ch"))
    last = n // 2 - 1
    piece, part = (pieces, group, depth, LANES), (pieces, group // 2, depth, LANES)
    slots = LOADS + AHEAD
    lhs = (group, 2, panel_len, depth * parts)
    return pl.pallas_call(
        functools.partial(spread_kernel, n, steps),
        in_specs=[pl.BlockSpec(memory_space=pl.ANY), pl.BlockSpec(memory_space=pl.ANY)],
        out_specs=[pl.BlockSpec(memory_space=pl.ANY)] * 7,
        out_shape=[
            jax.ShapeDtypeStruct(shape, jnp.bfloat16)
            for shape in (lhs, piece, (2 * (last - 1),) + piece) + (part,) * 4
        ],
        scratch_shapes=[
            pltpu.VMEM((taps_rows, span_len), jnp.bfloat16),
            pltpu.VMEM((slots, PART_STEPS // LOADS, LANES, span_len), jnp.bfloat16),
            pltpu.VMEM((2, TAPS - 1, LANES, span_len), jnp.bfloat16),
            pltpu.VMEM((PART_STEPS + TAPS - 1, taps_rows, LANES), jnp.float32),
            pltpu.VMEM((rows * PART_STEPS, LANES), jnp.float32),
            pltpu.VMEM((pieces, rows // 2, depth, LANES), jnp.bfloat16),
            pltpu.VMEM((pieces, 2 * group, depth, LANES), jnp.bfloat16),
            pltpu.VMEM(piece, jnp.bfloat16),
            pltpu.VMEM(piece, jnp.bfloat16),
            pltpu.VMEM(piece, jnp.bfloat16),
            pltpu.VMEM(lhs, jnp.bfloat16),
            pltpu.SemaphoreType.DMA,
            pltpu.SemaphoreType.DMA((slots,)),
            pltpu.SemaphoreType.DMA((2,)),
            pltpu.SemaphoreType.DMA((2, pieces)),
            pltpu.SemaphoreType.DMA((2, pieces)),
            pltpu.SemaphoreType.DMA((2, last - 1, pieces)),
            pltpu.SemaphoreType.DMA((2, last - 1, pieces)),
            pltpu.SemaphoreType.DMA((2, 2, pieces)),
            pltpu.SemaphoreType.DMA((2, 2, pieces)),
            pltpu.SemaphoreType.DMA((pieces,)),
            pltpu.SemaphoreType.DMA((panel_len // LANES,)),
        ],
        compiler_params=pltpu.CompilerParams(
            collective_id=0, has_side_effects=True, vmem_limit_bytes=SPREAD_VMEM
        ),
    )(voltages, table)


def make_rhs(parts, panel, c):
    pieces = panel.shape[0]
    return jnp.concatenate(
        [
            jnp.concatenate([panel[q * parts + part, c] for part in range(parts)], axis=0)
            for q in range(pieces // parts)
        ],
        axis=1,
    )


def halves_rhs(parts, low, high, c):
    half = low.shape[1]
    return jnp.where(
        c < half, make_rhs(parts, low, jnp.minimum(c, half - 1)), make_rhs(parts, high, jnp.maximum(c - half, 0))
    )


def pair_tile(lhs_ref, c, rhs, tile):
    _, _, panel_len, depth = lhs_ref.shape
    steps = depth // 2
    sums = jnp.dot(lhs_ref[c].reshape(2 * panel_len, depth), rhs, preferred_element_type=jnp.float32)
    scaled = (sums * (1.0 / steps)).astype(jnp.bfloat16)
    tile[0] = scaled[:panel_len]
    tile[1] = scaled[panel_len:]


def tile_copy(tile, out_ref, c, panel, sem):
    panel_len = tile.shape[1]
    columns = pl.ds(pl.multiple_of(panel * panel_len, panel_len), panel_len)
    return pltpu.make_async_copy(tile, out_ref.at[c, :, :, columns], sem)


def near_kernel(n, parts, lhs_ref, own_ref, near_ref, low0, high0, low1, high1, out_ref, tiles, sems):
    chans = lhs_ref.shape[0]
    place = place_of(lax.axis_index("blk"), n)
    last = n // 2 - 1
    makers = [(place, lambda c: make_rhs(parts, own_ref, c))]
    for slot in range(near_ref.shape[0]):
        hop, side = slot // 2 + 1, slot % 2
        makers.append((place - hop * (1 - 2 * side), lambda c, slot=slot: make_rhs(parts, near_ref.at[slot], c)))
    makers.append((place - last, lambda c: halves_rhs(parts, low0, high0, c)))
    makers.append((place + last, lambda c: halves_rhs(parts, low1, high1, c)))

    def copy(c, i):
        return tile_copy(tiles.at[i], out_ref, c, block_at(makers[i][0], n), sems.at[i])

    def one_channel(c, carry):
        for i, (_, rhs) in enumerate(makers):
            @pl.when(c > 0)
            def _():
                copy(c, i).wait()

            pair_tile(lhs_ref, c, rhs(c), tiles.at[i])
            copy(c, i).start()
        return carry

    lax.fori_loop(0, chans, one_channel, 0)
    for i in range(len(makers)):
        copy(0, i).wait()


def across_kernel(n, parts, lhs_ref, low, high, _, out_ref, tiles, sems):
    chans = lhs_ref.shape[0]
    panel = block_at(place_of(lax.axis_index("blk"), n) + n // 2, n)

    def copy(c):
        return tile_copy(tiles.at[c], out_ref, c, panel, sems.at[c])

    for c in range(chans):
        source, index = (low, c) if c < chans // 2 else (high, c - chans // 2)
        pair_tile(lhs_ref, c, make_rhs(parts, source, index), tiles.at[c])
        copy(c).start()
    for c in range(chans):
        copy(c).wait()


def correlate(kernel, count, parts, lhs, operands, visibilities=None):
    n = lax.axis_size("blk")
    chans, _, panel_len, depth = lhs.shape
    specs = [pl.BlockSpec(memory_space=pltpu.VMEM)] * (1 + len(operands))
    extra, aliases, buffers = [], {}, count
    if visibilities is not None:
        extra, aliases, buffers = [visibilities], {len(specs): 0}, chans
        specs = specs + [pl.BlockSpec(memory_space=pl.ANY)]
    tile_bytes = chans * count * 2 * panel_len * panel_len * 2
    return pl.pallas_call(
        functools.partial(kernel, n, parts),
        in_specs=specs,
        out_specs=pl.BlockSpec(memory_space=pl.ANY),
        out_shape=jax.ShapeDtypeStruct((chans, 2, panel_len, n * panel_len), jnp.bfloat16),
        input_output_aliases=aliases,
        scratch_shapes=[
            pltpu.VMEM((buffers, 2, panel_len, panel_len), jnp.bfloat16),
            pltpu.SemaphoreType.DMA((buffers,)),
        ],
        cost_estimate=pl.CostEstimate(
            flops=tile_bytes * depth, bytes_accessed=tile_bytes * 5 // 4, transcendentals=0
        ),
        compiler_params=pltpu.CompilerParams(vmem_limit_bytes=PAIR_VMEM),
    )(lhs, *operands, *extra)


def body(voltages):
    groups = lax.axis_size("sec") * lax.axis_size("ch")
    n = lax.axis_size("blk")
    parts = (voltages.shape[0] - TAPS + 1) // PART_STEPS
    lhs, own, near, low0, high0, low1, high1 = spread(voltages, jnp.asarray(make_weights(groups)))
    order = [2 * p if p < n // 2 else 2 * n - 1 - 2 * p for p in range(n)]
    low = lax.ppermute(low0, "blk", [(order[p], order[(p + 1) % n]) for p in range(n)])
    high = lax.ppermute(high1, "blk", [(order[p], order[(p - 1) % n]) for p in range(n)])
    visibilities = correlate(near_kernel, n - 1, parts, lhs, (own, near, low0, high0, low1, high1))
    return correlate(across_kernel, 1, parts, lhs, (low, high), visibilities)


def solution(mesh):
    return jax.shard_map(
        body,
        mesh=mesh,
        in_specs=(P(None, "blk", ("sec", "ch")),),
        out_specs=P(("sec", "ch"), None, "blk", None),
        check_vma=False,
    )
```

```python
import functools

import jax
import jax.numpy as jnp
import numpy as np
from jax import lax
from jax.experimental import pallas as pl
from jax.experimental.pallas import tpu as pltpu
from jax.sharding import PartitionSpec as P

FFT = 2048
NCHAN = 1024
TAPS = 4
CH_GRP = 4
LANES = 128
PART_STEPS = 24
LOADS = 4
LAG = 2
CHIP_LAG = 2
AHEAD = 4
SPREAD_VMEM = 40 * 1024 * 1024
PAIR_VMEM = 40 * 1024 * 1024
MESH = pl.DeviceIdType.MESH


def window_gain():
    position = np.arange(TAPS * FFT, dtype=np.float64)
    taper = 0.5 - 0.5 * np.cos(2.0 * np.pi * (position + 0.5) / (TAPS * FFT))
    profile = np.sinc((position - TAPS * FFT / 2 + 0.5) / FFT) * taper
    return float(np.sqrt(FFT / np.sum(profile * profile)))


def window_at(first, span_len):
    shape = (TAPS, span_len)
    sample = lax.broadcasted_iota(jnp.int32, shape, 1) + first
    position = (lax.broadcasted_iota(jnp.int32, shape, 0) * FFT + sample).astype(jnp.float32)
    angle = (np.pi / FFT) * (position - (TAPS * FFT / 2 - 0.5))
    taper = 0.5 - 0.5 * jnp.cos((2.0 * np.pi / (TAPS * FFT)) * (position + 0.5))
    return jnp.sin(angle) / angle * taper * window_gain()


def table_at(first, span_len, chan_total):
    spacing = NCHAN // chan_total
    assert LANES * (spacing // 2) % FFT == 0 and span_len % LANES == 0
    shape = (2 * chan_total, LANES)
    row = lax.broadcasted_iota(jnp.int32, shape, 0)
    sample = lax.broadcasted_iota(jnp.int32, shape, 1) + first
    chosen = row // 2 * spacing + spacing // 2
    phase = lax.rem(chosen * sample, FFT).astype(jnp.float32)
    angle = (2.0 * np.pi / FFT) * phase
    wave = jnp.where(lax.rem(row, 2) == 0, jnp.cos(angle), -jnp.sin(angle)) * float(1.0 / np.sqrt(FFT))
    wave = wave.astype(jnp.bfloat16).astype(jnp.float32)
    return jnp.concatenate([wave] * (span_len // LANES), axis=1)


def block_at(place, n):
    place = lax.rem(place + 2 * n, n)
    return 2 * place + place // (n // 2) * (2 * n - 1 - 4 * place)


def place_of(blk, n):
    return blk // 2 + lax.rem(blk, 2) * (n - 1 - 2 * (blk // 2))


def spread_kernel(n, steps, volts_ref, lhs_ref, tiles_ref, near_ref, low0, high0, low1, high1, weights, volts,
                  head, products, spectra, terms, got_core, half, got_chip, own, lhs, volts_sems, head_sems,
                  core_sems, chip_sems, near_send, near_recv, far_send, far_recv, lhs_sems):
    sec, ch, blk = lax.axis_index("sec"), lax.axis_index("ch"), lax.axis_index("blk")
    other_sec, other_ch = 1 - sec, 1 - ch
    pieces, group = own.shape[0], own.shape[1]
    far_refs = ((low0, high0), (low1, high1))
    last = n // 2 - 1
    part_len = products.shape[0] - (TAPS - 1)
    parts = steps // part_len
    rows = weights.shape[0] // TAPS
    slots = volts.shape[0]
    place = place_of(blk, n)
    sides = (block_at(place + 1, n), block_at(place - 1, n))

    def volts_copy(load):
        slot = lax.rem(load, slots)
        count = volts.shape[1]
        k = load // LOADS
        first = lax.rem(k, parts) * part_len + TAPS - 1 + lax.rem(load, LOADS) * count
        return pltpu.make_async_copy(
            volts_ref.at[pl.ds(first, count), pl.ds(k // parts * LANES, LANES)], volts.at[slot], volts_sems.at[slot]
        )

    def head_copy(q):
        slot = lax.rem(q, 2)
        return pltpu.make_async_copy(
            volts_ref.at[pl.ds(0, TAPS - 1), pl.ds(q * LANES, LANES)], head.at[slot], head_sems.at[slot]
        )

    def filtered(samples):
        return lax.dot_general(
            weights[...], samples, (((1,), (1,)), ((), ())), preferred_element_type=jnp.float32
        )

    def produce(k):
        part = lax.rem(k, parts)

        @pl.when(part == 0)
        def _():
            q = k // parts
            head_copy(q).wait()

            @pl.when(q + 1 < pieces // parts)
            def _():
                head_copy(q + 1).start()

            for frame in range(TAPS - 1):
                products[frame] = filtered(head[lax.rem(q, 2), frame])

        @pl.when(part > 0)
        def _():
            for frame in range(TAPS - 1):
                products[frame] = products[part_len + frame]

        count = volts.shape[1]
        for index in range(LOADS):
            load = k * LOADS + index
            volts_copy(load).wait()

            @pl.when(load + AHEAD < pieces * LOADS)
            def _():
                volts_copy(load + AHEAD).start()

            slot = lax.rem(load, slots)
            for frame in range(count):
                products[TAPS - 1 + index * count + frame] = filtered(volts[slot, frame])

        def add_taps(step, carry):
            total = products[step, 0:rows]
            for tap in range(1, TAPS):
                total = total + products[step + tap, tap * rows : (tap + 1) * rows]
            spectra[pl.ds(step, rows, stride=part_len), :] = total
            return carry

        lax.fori_loop(0, part_len, add_taps, 0, unroll=8)
        terms[k] = spectra[...].reshape(terms.shape[1:]).astype(jnp.bfloat16)

    def core_copy(k):
        return pltpu.make_async_remote_copy(
            src_ref=terms.at[k, pl.ds(other_sec * 2 * group, 2 * group)],
            dst_ref=got_core.at[k],
            send_sem=core_sems.at[0, k],
            recv_sem=core_sems.at[1, k],
            device_id={"sec": other_sec},
            device_id_type=MESH,
        )

    def chip_copy(k):
        return pltpu.make_async_remote_copy(
            src_ref=half.at[k],
            dst_ref=got_chip.at[k],
            send_sem=chip_sems.at[0, k],
            recv_sem=chip_sems.at[1, k],
            device_id={"ch": other_ch},
            device_id_type=MESH,
        )

    def ring_copies(k, side, hop):
        source = own.at[k] if hop == 1 else near_ref.at[2 * (hop - 2) + side, k]
        if hop < last:
            moves = [(source, near_ref.at[2 * (hop - 1) + side, k], near_send.at[side, hop - 1, k],
                      near_recv.at[side, hop - 1, k])]
        else:
            moves = [
                (source.at[pl.ds(part * (group // 2), group // 2)], far_refs[side][part].at[k],
                 far_send.at[side, part, k], far_recv.at[side, part, k])
                for part in range(2)
            ]
        return [
            pltpu.make_async_remote_copy(
                src_ref=src,
                dst_ref=dst,
                send_sem=send,
                recv_sem=recv,
                device_id={"blk": sides[side]},
                device_id_type=MESH,
            )
            for src, dst, send, recv in moves
        ]

    def pair_sum(k, start):
        mine = terms[k, pl.ds(sec * 2 * group + start, group)].astype(jnp.float32)
        return mine + got_core[k, pl.ds(start, group)].astype(jnp.float32)

    def lhs_copy(q):
        rows_of = pl.ds(q * LANES, LANES)
        return pltpu.make_async_copy(lhs.at[:, :, rows_of], lhs_ref.at[:, :, rows_of], lhs_sems.at[q])

    def turn(q):
        rows_of = pl.ds(pl.multiple_of(q * LANES, LANES), LANES)
        for c in range(group):
            straight, crossed = [], []
            for part in range(parts):
                values = own[q * parts + part, c].astype(jnp.float32)
                straight.append(values)
                crossed += [values[part_len:], -values[:part_len]]
            lhs[c, 0, rows_of, :] = jnp.concatenate(straight, axis=0).T.astype(jnp.bfloat16)
            lhs[c, 1, rows_of, :] = jnp.concatenate(crossed, axis=0).T.astype(jnp.bfloat16)
        lhs_copy(q).start()

    def over_cores(k):
        core_copy(k).wait_recv()
        half[k] = pair_sum(k, other_ch * group).astype(jnp.bfloat16)
        chip_copy(k).start()

    def over_chips(k):
        total = pair_sum(k, ch * group)
        chip_copy(k).wait_recv()
        own[k] = (total + got_chip[k].astype(jnp.float32)).astype(jnp.bfloat16)
        for side in range(2):
            for copy in ring_copies(k, side, 1):
                copy.start()

        @pl.when(lax.rem(k, parts) == parts - 1)
        def _():
            turn(k // parts)

    def forward(k, hop):
        for side in range(2):
            for copy in ring_copies(k, side, hop):
                copy.wait_recv()
            for copy in ring_copies(k, side, hop + 1):
                copy.start()

    def finish(k):
        core_copy(k).wait_send()
        chip_copy(k).wait_send()
        for side in range(2):
            for copy in ring_copies(k, side, last):
                copy.wait_recv()
            for hop in range(1, last + 1):
                for copy in ring_copies(k, side, hop):
                    copy.wait_send()

    def when_piece(k, act, *values):
        @pl.when((k >= 0) & (k < pieces))
        def _():
            act(k, *values)

    head_copy(0).start()
    for load in range(AHEAD):
        volts_copy(load).start()
    barrier = pltpu.get_barrier_semaphore()
    partners = ({"sec": other_sec}, {"ch": other_ch}, {"blk": sides[0]}, {"blk": sides[1]})
    for partner in partners:
        pl.semaphore_signal(barrier, inc=1, device_id=partner, device_id_type=MESH)
    span_len = weights.shape[1]
    first = (sec * lax.axis_size("ch") + ch) * span_len
    window, table = window_at(first, span_len), table_at(first, span_len, rows // 2)
    for tap in range(TAPS):
        weights[tap * rows : (tap + 1) * rows] = (window[tap : tap + 1] * table).astype(jnp.bfloat16)

    def one_step(step, carry):
        @pl.when(step < pieces)
        def _():
            produce(step)

            @pl.when(step == 0)
            def _():
                pl.semaphore_wait(barrier, len(partners))

            core_copy(step).start()

        when_piece(step - 1 - CHIP_LAG - LAG * last, finish)
        for hop in range(last - 1, 0, -1):
            when_piece(step - 1 - CHIP_LAG - LAG * hop, forward, hop)
        when_piece(step - 1 - CHIP_LAG, over_chips)
        when_piece(step - 1, over_cores)

        tile = step - pieces - 1 - CHIP_LAG

        @pl.when((tile >= 0) & (tile < group))
        def _():
            pair_tile(lhs, tile, make_rhs(parts, own, tile), tiles_ref.at[tile])

        return carry

    lax.fori_loop(0, pieces + 1 + CHIP_LAG + LAG * last, one_step, 0)
    for q in range(pieces // parts):
        lhs_copy(q).wait()


def spread(voltages):
    n = lax.axis_size("blk")
    frames, panel_len, span_len = voltages.shape
    steps = frames - TAPS + 1
    groups = lax.axis_size("sec") * lax.axis_size("ch")
    rows = 2 * CH_GRP * groups
    taps_rows = TAPS * rows
    parts = steps // PART_STEPS
    pieces, depth = panel_len // LANES * parts, 2 * PART_STEPS
    group = CH_GRP
    last = n // 2 - 1
    piece, part = (pieces, group, depth, LANES), (pieces, group // 2, depth, LANES)
    slots = LOADS + AHEAD
    lhs, tiles = (group, 2, panel_len, depth * parts), (group, 2, panel_len, panel_len)
    return pl.pallas_call(
        functools.partial(spread_kernel, n, steps),
        in_specs=[pl.BlockSpec(memory_space=pl.ANY)],
        out_specs=[pl.BlockSpec(memory_space=space) for space in (pl.ANY, pltpu.VMEM) + (pl.ANY,) * 5],
        out_shape=[
            jax.ShapeDtypeStruct(shape, jnp.bfloat16)
            for shape in (lhs, tiles, (2 * (last - 1),) + piece) + (part,) * 4
        ],
        scratch_shapes=[
            pltpu.VMEM((taps_rows, span_len), jnp.bfloat16),
            pltpu.VMEM((slots, PART_STEPS // LOADS, LANES, span_len), jnp.bfloat16),
            pltpu.VMEM((2, TAPS - 1, LANES, span_len), jnp.bfloat16),
            pltpu.VMEM((PART_STEPS + TAPS - 1, taps_rows, LANES), jnp.float32),
            pltpu.VMEM((rows * PART_STEPS, LANES), jnp.float32),
            pltpu.VMEM((pieces, rows // 2, depth, LANES), jnp.bfloat16),
            pltpu.VMEM((pieces, 2 * group, depth, LANES), jnp.bfloat16),
            pltpu.VMEM(piece, jnp.bfloat16),
            pltpu.VMEM(piece, jnp.bfloat16),
            pltpu.VMEM(piece, jnp.bfloat16),
            pltpu.VMEM(lhs, jnp.bfloat16),
            pltpu.SemaphoreType.DMA((slots,)),
            pltpu.SemaphoreType.DMA((2,)),
            pltpu.SemaphoreType.DMA((2, pieces)),
            pltpu.SemaphoreType.DMA((2, pieces)),
            pltpu.SemaphoreType.DMA((2, last - 1, pieces)),
            pltpu.SemaphoreType.DMA((2, last - 1, pieces)),
            pltpu.SemaphoreType.DMA((2, 2, pieces)),
            pltpu.SemaphoreType.DMA((2, 2, pieces)),
            pltpu.SemaphoreType.DMA((panel_len // LANES,)),
        ],
        compiler_params=pltpu.CompilerParams(
            collective_id=0, has_side_effects=True, vmem_limit_bytes=SPREAD_VMEM
        ),
    )(voltages)


def make_rhs(parts, panel, c):
    pieces = panel.shape[0]
    return jnp.concatenate(
        [
            jnp.concatenate([panel[q * parts + part, c] for part in range(parts)], axis=0)
            for q in range(pieces // parts)
        ],
        axis=1,
    )


def halves_rhs(parts, low, high, c):
    half = low.shape[1]
    return jnp.where(
        c < half, make_rhs(parts, low, jnp.minimum(c, half - 1)), make_rhs(parts, high, jnp.maximum(c - half, 0))
    )


def pair_tile(lhs_ref, c, rhs, tile):
    _, _, panel_len, depth = lhs_ref.shape
    steps = depth // 2
    sums = jnp.dot(lhs_ref[c].reshape(2 * panel_len, depth), rhs, preferred_element_type=jnp.float32)
    scaled = (sums * (1.0 / steps)).astype(jnp.bfloat16)
    tile[0] = scaled[:panel_len]
    tile[1] = scaled[panel_len:]


def tile_copy(tile, out_ref, c, panel, sem):
    panel_len = tile.shape[1]
    columns = pl.ds(pl.multiple_of(panel * panel_len, panel_len), panel_len)
    return pltpu.make_async_copy(tile, out_ref.at[c, :, :, columns], sem)


def near_kernel(n, parts, lhs_ref, own_ref, near_ref, low0, high0, low1, high1, out_ref, tiles, sems,
                own_sems):
    chans = lhs_ref.shape[0]
    place = place_of(lax.axis_index("blk"), n)
    last = n // 2 - 1
    makers = []
    for slot in range(near_ref.shape[0]):
        hop, side = slot // 2 + 1, slot % 2
        makers.append((place - hop * (1 - 2 * side), lambda c, slot=slot: make_rhs(parts, near_ref.at[slot], c)))
    makers.append((place - last, lambda c: halves_rhs(parts, low0, high0, c)))
    makers.append((place + last, lambda c: halves_rhs(parts, low1, high1, c)))

    def copy(c, i):
        return tile_copy(tiles.at[i], out_ref, c, block_at(makers[i][0], n), sems.at[i])

    def own_copy(c):
        return tile_copy(own_ref.at[c], out_ref, c, block_at(place, n), own_sems.at[c])

    for c in range(chans):
        own_copy(c).start()

    def one_channel(c, carry):
        for i, (_, rhs) in enumerate(makers):
            @pl.when(c > 0)
            def _():
                copy(c, i).wait()

            pair_tile(lhs_ref, c, rhs(c), tiles.at[i])
            copy(c, i).start()
        return carry

    lax.fori_loop(0, chans, one_channel, 0)
    for i in range(len(makers)):
        copy(0, i).wait()
    for c in range(chans):
        own_copy(c).wait()


def across_kernel(n, parts, lhs_ref, low, high, _, out_ref, tiles, sems):
    chans = lhs_ref.shape[0]
    panel = block_at(place_of(lax.axis_index("blk"), n) + n // 2, n)

    def copy(c):
        return tile_copy(tiles.at[c], out_ref, c, panel, sems.at[c])

    for c in range(chans):
        source, index = (low, c) if c < chans // 2 else (high, c - chans // 2)
        pair_tile(lhs_ref, c, make_rhs(parts, source, index), tiles.at[c])
        copy(c).start()
    for c in range(chans):
        copy(c).wait()


def correlate(kernel, count, parts, lhs, operands, visibilities=None):
    n = lax.axis_size("blk")
    chans, _, panel_len, depth = lhs.shape
    specs = [pl.BlockSpec(memory_space=pltpu.VMEM)] * (1 + len(operands))
    extra, aliases, buffers = [], {}, count
    if visibilities is not None:
        extra, aliases, buffers = [visibilities], {len(specs): 0}, chans
        specs = specs + [pl.BlockSpec(memory_space=pl.ANY)]
    tile_bytes = chans * count * 2 * panel_len * panel_len * 2
    return pl.pallas_call(
        functools.partial(kernel, n, parts),
        in_specs=specs,
        out_specs=pl.BlockSpec(memory_space=pl.ANY),
        out_shape=jax.ShapeDtypeStruct((chans, 2, panel_len, n * panel_len), jnp.bfloat16),
        input_output_aliases=aliases,
        scratch_shapes=[
            pltpu.VMEM((buffers, 2, panel_len, panel_len), jnp.bfloat16),
            pltpu.SemaphoreType.DMA((buffers,)),
        ]
        + [pltpu.SemaphoreType.DMA((chans,))] * (visibilities is None),
        cost_estimate=pl.CostEstimate(
            flops=tile_bytes * depth, bytes_accessed=tile_bytes * 5 // 4, transcendentals=0
        ),
        compiler_params=pltpu.CompilerParams(vmem_limit_bytes=PAIR_VMEM),
    )(lhs, *operands, *extra)


def body(voltages):
    n = lax.axis_size("blk")
    parts = (voltages.shape[0] - TAPS + 1) // PART_STEPS
    lhs, tiles, near, low0, high0, low1, high1 = spread(voltages)
    order = [2 * p if p < n // 2 else 2 * n - 1 - 2 * p for p in range(n)]
    low = lax.ppermute(low0, "blk", [(order[p], order[(p + 1) % n]) for p in range(n)])
    high = lax.ppermute(high1, "blk", [(order[p], order[(p - 1) % n]) for p in range(n)])
    visibilities = correlate(near_kernel, n - 2, parts, lhs, (tiles, near, low0, high0, low1, high1))
    return correlate(across_kernel, 1, parts, lhs, (low, high), visibilities)


def solution(mesh):
    return jax.shard_map(
        body,
        mesh=mesh,
        in_specs=(P(None, "blk", ("sec", "ch")),),
        out_specs=P(("sec", "ch"), None, "blk", None),
        check_vma=False,
    )
```

```python
import functools

import jax
import jax.numpy as jnp
import numpy as np
from jax import lax
from jax.experimental import pallas as pl
from jax.experimental.pallas import tpu as pltpu
from jax.sharding import PartitionSpec as P

FFT = 2048
NCHAN = 1024
TAPS = 4
CH_GRP = 4
LANES = 128
PART_STEPS = 24
LOADS = 2
LAG = 2
CHIP_LAG = 2
AHEAD = 2
SPREAD_VMEM = 40 * 1024 * 1024
PAIR_VMEM = 40 * 1024 * 1024
MESH = pl.DeviceIdType.MESH


def window_gain():
    position = np.arange(TAPS * FFT, dtype=np.float64)
    taper = 0.5 - 0.5 * np.cos(2.0 * np.pi * (position + 0.5) / (TAPS * FFT))
    profile = np.sinc((position - TAPS * FFT / 2 + 0.5) / FFT) * taper
    return float(np.sqrt(FFT / np.sum(profile * profile)))


def window_at(first, span_len):
    shape = (TAPS, span_len)
    sample = lax.broadcasted_iota(jnp.int32, shape, 1) + first
    position = (lax.broadcasted_iota(jnp.int32, shape, 0) * FFT + sample).astype(jnp.float32)
    angle = (np.pi / FFT) * (position - (TAPS * FFT / 2 - 0.5))
    taper = 0.5 - 0.5 * jnp.cos((2.0 * np.pi / (TAPS * FFT)) * (position + 0.5))
    return jnp.sin(angle) / angle * taper * window_gain()


def table_at(first, span_len, chan_total):
    spacing = NCHAN // chan_total
    assert LANES * (spacing // 2) % FFT == 0 and span_len % LANES == 0
    shape = (2 * chan_total, LANES)
    row = lax.broadcasted_iota(jnp.int32, shape, 0)
    sample = lax.broadcasted_iota(jnp.int32, shape, 1) + first
    chosen = row // 2 * spacing + spacing // 2
    phase = lax.rem(chosen * sample, FFT).astype(jnp.float32)
    angle = (2.0 * np.pi / FFT) * phase
    wave = jnp.where(lax.rem(row, 2) == 0, jnp.cos(angle), -jnp.sin(angle)) * float(1.0 / np.sqrt(FFT))
    wave = wave.astype(jnp.bfloat16).astype(jnp.float32)
    return jnp.concatenate([wave] * (span_len // LANES), axis=1)


def block_at(place, n):
    place = lax.rem(place + 2 * n, n)
    return 2 * place + place // (n // 2) * (2 * n - 1 - 4 * place)


def place_of(blk, n):
    return blk // 2 + lax.rem(blk, 2) * (n - 1 - 2 * (blk // 2))


def spread_kernel(n, steps, volts_ref, lhs_ref, tiles_ref, near_ref, low0, high0, low1, high1, weights, volts,
                  head, products, spectra, terms, got_core, half, got_chip, own, lhs, volts_sems, head_sems,
                  core_sems, chip_sems, near_send, near_recv, far_send, far_recv, lhs_sems):
    sec, ch, blk = lax.axis_index("sec"), lax.axis_index("ch"), lax.axis_index("blk")
    other_sec, other_ch = 1 - sec, 1 - ch
    pieces, group = own.shape[0], own.shape[1]
    far_refs = ((low0, high0), (low1, high1))
    last = n // 2 - 1
    part_len = products.shape[0] - (TAPS - 1)
    parts = steps // part_len
    rows = weights.shape[0] // TAPS
    slots = volts.shape[0]
    place = place_of(blk, n)
    sides = (block_at(place + 1, n), block_at(place - 1, n))

    def volts_copy(load):
        slot = lax.rem(load, slots)
        count = volts.shape[1]
        k = load // LOADS
        first = lax.rem(k, parts) * part_len + TAPS - 1 + lax.rem(load, LOADS) * count
        return pltpu.make_async_copy(
            volts_ref.at[pl.ds(first, count), pl.ds(k // parts * LANES, LANES)], volts.at[slot], volts_sems.at[slot]
        )

    def head_copy(q):
        slot = lax.rem(q, 2)
        return pltpu.make_async_copy(
            volts_ref.at[pl.ds(0, TAPS - 1), pl.ds(q * LANES, LANES)], head.at[slot], head_sems.at[slot]
        )

    def filtered(samples):
        return lax.dot_general(
            weights[...], samples, (((1,), (1,)), ((), ())), preferred_element_type=jnp.float32
        )

    def produce(k):
        part = lax.rem(k, parts)

        @pl.when(part == 0)
        def _():
            q = k // parts
            head_copy(q).wait()

            @pl.when(q + 1 < pieces // parts)
            def _():
                head_copy(q + 1).start()

            for frame in range(TAPS - 1):
                products[frame] = filtered(head[lax.rem(q, 2), frame])

        @pl.when(part > 0)
        def _():
            for frame in range(TAPS - 1):
                products[frame] = products[part_len + frame]

        count = volts.shape[1]
        for index in range(LOADS):
            load = k * LOADS + index
            volts_copy(load).wait()

            @pl.when(load + AHEAD < pieces * LOADS)
            def _():
                volts_copy(load + AHEAD).start()

            slot = lax.rem(load, slots)
            for frame in range(count):
                products[TAPS - 1 + index * count + frame] = filtered(volts[slot, frame])

        def add_taps(step, carry):
            total = products[step, 0:rows]
            for tap in range(1, TAPS):
                total = total + products[step + tap, tap * rows : (tap + 1) * rows]
            spectra[pl.ds(step, rows, stride=part_len), :] = total
            return carry

        lax.fori_loop(0, part_len, add_taps, 0, unroll=8)
        terms[k] = spectra[...].reshape(terms.shape[1:]).astype(jnp.bfloat16)

    def core_copy(k):
        return pltpu.make_async_remote_copy(
            src_ref=terms.at[k, pl.ds(other_sec * 2 * group, 2 * group)],
            dst_ref=got_core.at[k],
            send_sem=core_sems.at[0, k],
            recv_sem=core_sems.at[1, k],
            device_id={"sec": other_sec},
            device_id_type=MESH,
        )

    def chip_copy(k):
        return pltpu.make_async_remote_copy(
            src_ref=half.at[k],
            dst_ref=got_chip.at[k],
            send_sem=chip_sems.at[0, k],
            recv_sem=chip_sems.at[1, k],
            device_id={"ch": other_ch},
            device_id_type=MESH,
        )

    def ring_copies(k, side, hop):
        source = own.at[k] if hop == 1 else near_ref.at[2 * (hop - 2) + side, k]
        if hop < last:
            moves = [(source, near_ref.at[2 * (hop - 1) + side, k], near_send.at[side, hop - 1, k],
                      near_recv.at[side, hop - 1, k])]
        else:
            moves = [
                (source.at[pl.ds(part * (group // 2), group // 2)], far_refs[side][part].at[k],
                 far_send.at[side, part, k], far_recv.at[side, part, k])
                for part in range(2)
            ]
        return [
            pltpu.make_async_remote_copy(
                src_ref=src,
                dst_ref=dst,
                send_sem=send,
                recv_sem=recv,
                device_id={"blk": sides[side]},
                device_id_type=MESH,
            )
            for src, dst, send, recv in moves
        ]

    def pair_sum(k, start):
        mine = terms[k, pl.ds(sec * 2 * group + start, group)].astype(jnp.float32)
        return mine + got_core[k, pl.ds(start, group)].astype(jnp.float32)

    def lhs_copy(q):
        rows_of = pl.ds(q * LANES, LANES)
        return pltpu.make_async_copy(lhs.at[:, :, rows_of], lhs_ref.at[:, :, rows_of], lhs_sems.at[q])

    def turn(q):
        rows_of = pl.ds(pl.multiple_of(q * LANES, LANES), LANES)
        for c in range(group):
            straight, crossed = [], []
            for part in range(parts):
                values = own[q * parts + part, c].astype(jnp.float32)
                straight.append(values)
                crossed += [values[part_len:], -values[:part_len]]
            lhs[c, 0, rows_of, :] = jnp.concatenate(straight, axis=0).T.astype(jnp.bfloat16)
            lhs[c, 1, rows_of, :] = jnp.concatenate(crossed, axis=0).T.astype(jnp.bfloat16)
        lhs_copy(q).start()

    def over_cores(k):
        core_copy(k).wait_recv()
        half[k] = pair_sum(k, other_ch * group).astype(jnp.bfloat16)
        chip_copy(k).start()

    def over_chips(k):
        total = pair_sum(k, ch * group)
        chip_copy(k).wait_recv()
        own[k] = (total + got_chip[k].astype(jnp.float32)).astype(jnp.bfloat16)
        for side in range(2):
            for copy in ring_copies(k, side, 1):
                copy.start()

        @pl.when(lax.rem(k, parts) == parts - 1)
        def _():
            turn(k // parts)

    def forward(k, hop):
        for side in range(2):
            for copy in ring_copies(k, side, hop):
                copy.wait_recv()
            for copy in ring_copies(k, side, hop + 1):
                copy.start()

    def finish(k):
        core_copy(k).wait_send()
        chip_copy(k).wait_send()
        for side in range(2):
            for copy in ring_copies(k, side, last):
                copy.wait_recv()
            for hop in range(1, last + 1):
                for copy in ring_copies(k, side, hop):
                    copy.wait_send()

    def when_piece(k, act, *values):
        @pl.when((k >= 0) & (k < pieces))
        def _():
            act(k, *values)

    head_copy(0).start()
    for load in range(AHEAD):
        volts_copy(load).start()
    barrier = pltpu.get_barrier_semaphore()
    partners = ({"sec": other_sec}, {"ch": other_ch}, {"blk": sides[0]}, {"blk": sides[1]})
    for partner in partners:
        pl.semaphore_signal(barrier, inc=1, device_id=partner, device_id_type=MESH)
    span_len = weights.shape[1]
    first = (sec * lax.axis_size("ch") + ch) * span_len
    window, table = window_at(first, span_len), table_at(first, span_len, rows // 2)
    for tap in range(TAPS):
        weights[tap * rows : (tap + 1) * rows] = (window[tap : tap + 1] * table).astype(jnp.bfloat16)

    def one_step(step, carry):
        @pl.when(step < pieces)
        def _():
            produce(step)

            @pl.when(step == 0)
            def _():
                pl.semaphore_wait(barrier, len(partners))

            core_copy(step).start()

        when_piece(step - 1 - CHIP_LAG - LAG * last, finish)
        for hop in range(last - 1, 0, -1):
            when_piece(step - 1 - CHIP_LAG - LAG * hop, forward, hop)
        when_piece(step - 1 - CHIP_LAG, over_chips)
        when_piece(step - 1, over_cores)

        tile = step - pieces - 1 - CHIP_LAG

        @pl.when((tile >= 0) & (tile < group))
        def _():
            pair_tile(lhs, tile, make_rhs(parts, own, tile), tiles_ref.at[tile])

        return carry

    lax.fori_loop(0, pieces + 1 + CHIP_LAG + LAG * last, one_step, 0)
    for q in range(pieces // parts):
        lhs_copy(q).wait()


def spread(voltages):
    n = lax.axis_size("blk")
    frames, panel_len, span_len = voltages.shape
    steps = frames - TAPS + 1
    groups = lax.axis_size("sec") * lax.axis_size("ch")
    rows = 2 * CH_GRP * groups
    taps_rows = TAPS * rows
    parts = steps // PART_STEPS
    pieces, depth = panel_len // LANES * parts, 2 * PART_STEPS
    group = CH_GRP
    last = n // 2 - 1
    piece, part = (pieces, group, depth, LANES), (pieces, group // 2, depth, LANES)
    slots = LOADS + AHEAD
    lhs, tiles = (group, 2, panel_len, depth * parts), (group, 2, panel_len, panel_len)
    return pl.pallas_call(
        functools.partial(spread_kernel, n, steps),
        in_specs=[pl.BlockSpec(memory_space=pl.ANY)],
        out_specs=[pl.BlockSpec(memory_space=space) for space in (pl.ANY, pltpu.VMEM) + (pl.ANY,) * 5],
        out_shape=[
            jax.ShapeDtypeStruct(shape, jnp.bfloat16)
            for shape in (lhs, tiles, (2 * (last - 1),) + piece) + (part,) * 4
        ],
        scratch_shapes=[
            pltpu.VMEM((taps_rows, span_len), jnp.bfloat16),
            pltpu.VMEM((slots, PART_STEPS // LOADS, LANES, span_len), jnp.bfloat16),
            pltpu.VMEM((2, TAPS - 1, LANES, span_len), jnp.bfloat16),
            pltpu.VMEM((PART_STEPS + TAPS - 1, taps_rows, LANES), jnp.float32),
            pltpu.VMEM((rows * PART_STEPS, LANES), jnp.float32),
            pltpu.VMEM((pieces, rows // 2, depth, LANES), jnp.bfloat16),
            pltpu.VMEM((pieces, 2 * group, depth, LANES), jnp.bfloat16),
            pltpu.VMEM(piece, jnp.bfloat16),
            pltpu.VMEM(piece, jnp.bfloat16),
            pltpu.VMEM(piece, jnp.bfloat16),
            pltpu.VMEM(lhs, jnp.bfloat16),
            pltpu.SemaphoreType.DMA((slots,)),
            pltpu.SemaphoreType.DMA((2,)),
            pltpu.SemaphoreType.DMA((2, pieces)),
            pltpu.SemaphoreType.DMA((2, pieces)),
            pltpu.SemaphoreType.DMA((2, last - 1, pieces)),
            pltpu.SemaphoreType.DMA((2, last - 1, pieces)),
            pltpu.SemaphoreType.DMA((2, 2, pieces)),
            pltpu.SemaphoreType.DMA((2, 2, pieces)),
            pltpu.SemaphoreType.DMA((panel_len // LANES,)),
        ],
        compiler_params=pltpu.CompilerParams(
            collective_id=0, has_side_effects=True, vmem_limit_bytes=SPREAD_VMEM
        ),
    )(voltages)


def make_rhs(parts, panel, c):
    pieces = panel.shape[0]
    return jnp.concatenate(
        [
            jnp.concatenate([panel[q * parts + part, c] for part in range(parts)], axis=0)
            for q in range(pieces // parts)
        ],
        axis=1,
    )


def halves_rhs(parts, low, high, c):
    half = low.shape[1]
    return jnp.where(
        c < half, make_rhs(parts, low, jnp.minimum(c, half - 1)), make_rhs(parts, high, jnp.maximum(c - half, 0))
    )


def pair_tile(lhs_ref, c, rhs, tile):
    _, _, panel_len, depth = lhs_ref.shape
    steps = depth // 2
    sums = jnp.dot(lhs_ref[c].reshape(2 * panel_len, depth), rhs, preferred_element_type=jnp.float32)
    scaled = (sums * (1.0 / steps)).astype(jnp.bfloat16)
    tile[0] = scaled[:panel_len]
    tile[1] = scaled[panel_len:]


def tile_copy(tile, out_ref, c, panel, sem):
    panel_len = tile.shape[1]
    columns = pl.ds(pl.multiple_of(panel * panel_len, panel_len), panel_len)
    return pltpu.make_async_copy(tile, out_ref.at[c, :, :, columns], sem)


def near_kernel(n, parts, lhs_ref, own_ref, near_ref, low0, high0, low1, high1, out_ref, tiles, sems,
                own_sems):
    chans = lhs_ref.shape[0]
    place = place_of(lax.axis_index("blk"), n)
    last = n // 2 - 1
    makers = []
    for slot in range(near_ref.shape[0]):
        hop, side = slot // 2 + 1, slot % 2
        makers.append((place - hop * (1 - 2 * side), lambda c, slot=slot: make_rhs(parts, near_ref.at[slot], c)))
    makers.append((place - last, lambda c: halves_rhs(parts, low0, high0, c)))
    makers.append((place + last, lambda c: halves_rhs(parts, low1, high1, c)))

    def copy(c, i):
        return tile_copy(tiles.at[i], out_ref, c, block_at(makers[i][0], n), sems.at[i])

    def own_copy(c):
        return tile_copy(own_ref.at[c], out_ref, c, block_at(place, n), own_sems.at[c])

    for c in range(chans):
        own_copy(c).start()

    def one_channel(c, carry):
        for i, (_, rhs) in enumerate(makers):
            @pl.when(c > 0)
            def _():
                copy(c, i).wait()

            pair_tile(lhs_ref, c, rhs(c), tiles.at[i])
            copy(c, i).start()
        return carry

    lax.fori_loop(0, chans, one_channel, 0)
    for i in range(len(makers)):
        copy(0, i).wait()
    for c in range(chans):
        own_copy(c).wait()


def across_kernel(n, parts, lhs_ref, low, high, _, out_ref, tiles, sems):
    chans = lhs_ref.shape[0]
    panel = block_at(place_of(lax.axis_index("blk"), n) + n // 2, n)

    def copy(c):
        return tile_copy(tiles.at[c], out_ref, c, panel, sems.at[c])

    for c in range(chans):
        source, index = (low, c) if c < chans // 2 else (high, c - chans // 2)
        pair_tile(lhs_ref, c, make_rhs(parts, source, index), tiles.at[c])
        copy(c).start()
    for c in range(chans):
        copy(c).wait()


def correlate(kernel, count, parts, lhs, operands, visibilities=None):
    n = lax.axis_size("blk")
    chans, _, panel_len, depth = lhs.shape
    specs = [pl.BlockSpec(memory_space=pltpu.VMEM)] * (1 + len(operands))
    extra, aliases, buffers = [], {}, count
    if visibilities is not None:
        extra, aliases, buffers = [visibilities], {len(specs): 0}, chans
        specs = specs + [pl.BlockSpec(memory_space=pl.ANY)]
    tile_bytes = chans * count * 2 * panel_len * panel_len * 2
    return pl.pallas_call(
        functools.partial(kernel, n, parts),
        in_specs=specs,
        out_specs=pl.BlockSpec(memory_space=pl.ANY),
        out_shape=jax.ShapeDtypeStruct((chans, 2, panel_len, n * panel_len), jnp.bfloat16),
        input_output_aliases=aliases,
        scratch_shapes=[
            pltpu.VMEM((buffers, 2, panel_len, panel_len), jnp.bfloat16),
            pltpu.SemaphoreType.DMA((buffers,)),
        ]
        + [pltpu.SemaphoreType.DMA((chans,))] * (visibilities is None),
        cost_estimate=pl.CostEstimate(
            flops=tile_bytes * depth, bytes_accessed=tile_bytes * 5 // 4, transcendentals=0
        ),
        compiler_params=pltpu.CompilerParams(vmem_limit_bytes=PAIR_VMEM),
    )(lhs, *operands, *extra)


def body(voltages):
    n = lax.axis_size("blk")
    parts = (voltages.shape[0] - TAPS + 1) // PART_STEPS
    lhs, tiles, near, low0, high0, low1, high1 = spread(voltages)
    order = [2 * p if p < n // 2 else 2 * n - 1 - 2 * p for p in range(n)]
    low = lax.ppermute(low0, "blk", [(order[p], order[(p + 1) % n]) for p in range(n)])
    high = lax.ppermute(high1, "blk", [(order[p], order[(p - 1) % n]) for p in range(n)])
    visibilities = correlate(near_kernel, n - 2, parts, lhs, (tiles, near, low0, high0, low1, high1))
    return correlate(across_kernel, 1, parts, lhs, (low, high), visibilities)


def solution(mesh):
    return jax.shard_map(
        body,
        mesh=mesh,
        in_specs=(P(None, "blk", ("sec", "ch")),),
        out_specs=P(("sec", "ch"), None, "blk", None),
        check_vma=False,
    )
```

```python
import functools

import jax
import jax.numpy as jnp
import numpy as np
from jax import lax
from jax.experimental import pallas as pl
from jax.experimental.pallas import tpu as pltpu
from jax.sharding import PartitionSpec as P

FFT = 2048
NCHAN = 1024
TAPS = 4
CH_GRP = 4
LANES = 128
PART_STEPS = 24
LOADS = 2
LAG = 2
CHIP_LAG = 2
AHEAD = 2
SPREAD_VMEM = 40 * 1024 * 1024
PAIR_VMEM = 40 * 1024 * 1024
MESH = pl.DeviceIdType.MESH


def window_gain():
    position = np.arange(TAPS * FFT, dtype=np.float64)
    taper = 0.5 - 0.5 * np.cos(2.0 * np.pi * (position + 0.5) / (TAPS * FFT))
    profile = np.sinc((position - TAPS * FFT / 2 + 0.5) / FFT) * taper
    return float(np.sqrt(FFT / np.sum(profile * profile)))


def window_at(first, span_len):
    shape = (TAPS, span_len)
    sample = lax.broadcasted_iota(jnp.int32, shape, 1) + first
    position = (lax.broadcasted_iota(jnp.int32, shape, 0) * FFT + sample).astype(jnp.float32)
    angle = (np.pi / FFT) * (position - (TAPS * FFT / 2 - 0.5))
    taper = 0.5 - 0.5 * jnp.cos((2.0 * np.pi / (TAPS * FFT)) * (position + 0.5))
    return jnp.sin(angle) / angle * taper * window_gain()


def table_at(first, span_len, chan_total):
    spacing = NCHAN // chan_total
    assert LANES * (spacing // 2) % FFT == 0 and span_len % LANES == 0
    shape = (2 * chan_total, LANES)
    row = lax.broadcasted_iota(jnp.int32, shape, 0)
    sample = lax.broadcasted_iota(jnp.int32, shape, 1) + first
    chosen = row // 2 * spacing + spacing // 2
    phase = lax.rem(chosen * sample, FFT).astype(jnp.float32)
    angle = (2.0 * np.pi / FFT) * phase
    wave = jnp.where(lax.rem(row, 2) == 0, jnp.cos(angle), -jnp.sin(angle)) * float(1.0 / np.sqrt(FFT))
    wave = wave.astype(jnp.bfloat16).astype(jnp.float32)
    return jnp.concatenate([wave] * (span_len // LANES), axis=1)


def block_at(place, n):
    place = lax.rem(place + 2 * n, n)
    return 2 * place + place // (n // 2) * (2 * n - 1 - 4 * place)


def place_of(blk, n):
    return blk // 2 + lax.rem(blk, 2) * (n - 1 - 2 * (blk // 2))


def spread_kernel(n, steps, volts_ref, lhs_ref, tiles_ref, near_ref, low0, high0, low1, high1, weights, volts,
                  head, products, spectra, terms, got_core, half, got_chip, own, lhs, volts_sems, head_sems,
                  core_sems, chip_sems, near_send, near_recv, far_send, far_recv, lhs_sems):
    sec, ch, blk = lax.axis_index("sec"), lax.axis_index("ch"), lax.axis_index("blk")
    other_sec, other_ch = 1 - sec, 1 - ch
    pieces, group = own.shape[0], own.shape[1]
    far_refs = ((low0, high0), (low1, high1))
    last = n // 2 - 1
    part_len = products.shape[0] - (TAPS - 1)
    parts = steps // part_len
    rows = weights.shape[0] // TAPS
    slots = volts.shape[0]
    place = place_of(blk, n)
    sides = (block_at(place + 1, n), block_at(place - 1, n))

    def volts_copy(load):
        slot = lax.rem(load, slots)
        count = volts.shape[1]
        k = load // LOADS
        first = lax.rem(k, parts) * part_len + TAPS - 1 + lax.rem(load, LOADS) * count
        return pltpu.make_async_copy(
            volts_ref.at[pl.ds(first, count), pl.ds(k // parts * LANES, LANES)], volts.at[slot], volts_sems.at[slot]
        )

    def head_copy(q):
        slot = lax.rem(q, 2)
        return pltpu.make_async_copy(
            volts_ref.at[pl.ds(0, TAPS - 1), pl.ds(q * LANES, LANES)], head.at[slot], head_sems.at[slot]
        )

    def filtered(samples):
        return lax.dot_general(
            weights[...], samples, (((1,), (1,)), ((), ())), preferred_element_type=jnp.float32
        )

    def produce(k):
        part = lax.rem(k, parts)

        @pl.when(part == 0)
        def _():
            q = k // parts
            head_copy(q).wait()

            @pl.when(q + 1 < pieces // parts)
            def _():
                head_copy(q + 1).start()

            for frame in range(TAPS - 1):
                products[frame] = filtered(head[lax.rem(q, 2), frame])

        @pl.when(part > 0)
        def _():
            for frame in range(TAPS - 1):
                products[frame] = products[part_len + frame]

        count = volts.shape[1]
        for index in range(LOADS):
            load = k * LOADS + index
            volts_copy(load).wait()

            @pl.when(load + AHEAD < pieces * LOADS)
            def _():
                volts_copy(load + AHEAD).start()

            slot = lax.rem(load, slots)
            for frame in range(count):
                products[TAPS - 1 + index * count + frame] = filtered(volts[slot, frame])

        def add_taps(step, carry):
            total = products[step, 0:rows]
            for tap in range(1, TAPS):
                total = total + products[step + tap, tap * rows : (tap + 1) * rows]
            spectra[pl.ds(step, rows, stride=part_len), :] = total
            return carry

        lax.fori_loop(0, part_len, add_taps, 0, unroll=part_len)
        terms[k] = spectra[...].reshape(terms.shape[1:]).astype(jnp.bfloat16)

    def core_copy(k):
        return pltpu.make_async_remote_copy(
            src_ref=terms.at[k, pl.ds(other_sec * 2 * group, 2 * group)],
            dst_ref=got_core.at[k],
            send_sem=core_sems.at[0, k],
            recv_sem=core_sems.at[1, k],
            device_id={"sec": other_sec},
            device_id_type=MESH,
        )

    def chip_copy(k):
        return pltpu.make_async_remote_copy(
            src_ref=half.at[k],
            dst_ref=got_chip.at[k],
            send_sem=chip_sems.at[0, k],
            recv_sem=chip_sems.at[1, k],
            device_id={"ch": other_ch},
            device_id_type=MESH,
        )

    def ring_copies(k, side, hop):
        source = own.at[k] if hop == 1 else near_ref.at[2 * (hop - 2) + side, k]
        if hop < last:
            moves = [(source, near_ref.at[2 * (hop - 1) + side, k], near_send.at[side, hop - 1, k],
                      near_recv.at[side, hop - 1, k])]
        else:
            moves = [
                (source.at[pl.ds(part * (group // 2), group // 2)], far_refs[side][part].at[k],
                 far_send.at[side, part, k], far_recv.at[side, part, k])
                for part in range(2)
            ]
        return [
            pltpu.make_async_remote_copy(
                src_ref=src,
                dst_ref=dst,
                send_sem=send,
                recv_sem=recv,
                device_id={"blk": sides[side]},
                device_id_type=MESH,
            )
            for src, dst, send, recv in moves
        ]

    def pair_sum(k, start):
        mine = terms[k, pl.ds(sec * 2 * group + start, group)].astype(jnp.float32)
        return mine + got_core[k, pl.ds(start, group)].astype(jnp.float32)

    def lhs_copy(q):
        rows_of = pl.ds(q * LANES, LANES)
        return pltpu.make_async_copy(lhs.at[:, :, rows_of], lhs_ref.at[:, :, rows_of], lhs_sems.at[q])

    def turn(q):
        rows_of = pl.ds(pl.multiple_of(q * LANES, LANES), LANES)
        for c in range(group):
            straight, crossed = [], []
            for part in range(parts):
                values = own[q * parts + part, c].astype(jnp.float32)
                straight.append(values)
                crossed += [values[part_len:], -values[:part_len]]
            lhs[c, 0, rows_of, :] = jnp.concatenate(straight, axis=0).T.astype(jnp.bfloat16)
            lhs[c, 1, rows_of, :] = jnp.concatenate(crossed, axis=0).T.astype(jnp.bfloat16)
        lhs_copy(q).start()

    def over_cores(k):
        core_copy(k).wait_recv()
        half[k] = pair_sum(k, other_ch * group).astype(jnp.bfloat16)
        chip_copy(k).start()

    def over_chips(k):
        total = pair_sum(k, ch * group)
        chip_copy(k).wait_recv()
        own[k] = (total + got_chip[k].astype(jnp.float32)).astype(jnp.bfloat16)
        for side in range(2):
            for copy in ring_copies(k, side, 1):
                copy.start()

        @pl.when(lax.rem(k, parts) == parts - 1)
        def _():
            turn(k // parts)

    def forward(k, hop):
        for side in range(2):
            for copy in ring_copies(k, side, hop):
                copy.wait_recv()
            for copy in ring_copies(k, side, hop + 1):
                copy.start()

    def finish(k):
        core_copy(k).wait_send()
        chip_copy(k).wait_send()
        for side in range(2):
            for copy in ring_copies(k, side, last):
                copy.wait_recv()
            for hop in range(1, last + 1):
                for copy in ring_copies(k, side, hop):
                    copy.wait_send()

    def when_piece(k, act, *values):
        @pl.when((k >= 0) & (k < pieces))
        def _():
            act(k, *values)

    head_copy(0).start()
    for load in range(AHEAD):
        volts_copy(load).start()
    barrier = pltpu.get_barrier_semaphore()
    partners = ({"sec": other_sec}, {"ch": other_ch}, {"blk": sides[0]}, {"blk": sides[1]})
    for partner in partners:
        pl.semaphore_signal(barrier, inc=1, device_id=partner, device_id_type=MESH)
    span_len = weights.shape[1]
    first = (sec * lax.axis_size("ch") + ch) * span_len
    window, table = window_at(first, span_len), table_at(first, span_len, rows // 2)
    for tap in range(TAPS):
        weights[tap * rows : (tap + 1) * rows] = (window[tap : tap + 1] * table).astype(jnp.bfloat16)

    def one_step(step, carry):
        @pl.when(step < pieces)
        def _():
            produce(step)

            @pl.when(step == 0)
            def _():
                pl.semaphore_wait(barrier, len(partners))

            core_copy(step).start()

        when_piece(step - 1 - CHIP_LAG - LAG * last, finish)
        for hop in range(last - 1, 0, -1):
            when_piece(step - 1 - CHIP_LAG - LAG * hop, forward, hop)
        when_piece(step - 1 - CHIP_LAG, over_chips)
        when_piece(step - 1, over_cores)

        tile = step - pieces - 1 - CHIP_LAG

        @pl.when((tile >= 0) & (tile < group))
        def _():
            pair_tile(lhs, tile, make_rhs(parts, own, tile), tiles_ref.at[tile])

        return carry

    lax.fori_loop(0, pieces + 1 + CHIP_LAG + LAG * last, one_step, 0)
    for q in range(pieces // parts):
        lhs_copy(q).wait()


def spread(voltages):
    n = lax.axis_size("blk")
    frames, panel_len, span_len = voltages.shape
    steps = frames - TAPS + 1
    groups = lax.axis_size("sec") * lax.axis_size("ch")
    rows = 2 * CH_GRP * groups
    taps_rows = TAPS * rows
    parts = steps // PART_STEPS
    pieces, depth = panel_len // LANES * parts, 2 * PART_STEPS
    group = CH_GRP
    last = n // 2 - 1
    piece, part = (pieces, group, depth, LANES), (pieces, group // 2, depth, LANES)
    slots = LOADS + AHEAD
    lhs, tiles = (group, 2, panel_len, depth * parts), (group, 2, panel_len, panel_len)
    return pl.pallas_call(
        functools.partial(spread_kernel, n, steps),
        in_specs=[pl.BlockSpec(memory_space=pl.ANY)],
        out_specs=[pl.BlockSpec(memory_space=space) for space in (pl.ANY, pltpu.VMEM) + (pl.ANY,) * 5],
        out_shape=[
            jax.ShapeDtypeStruct(shape, jnp.bfloat16)
            for shape in (lhs, tiles, (2 * (last - 1),) + piece) + (part,) * 4
        ],
        scratch_shapes=[
            pltpu.VMEM((taps_rows, span_len), jnp.bfloat16),
            pltpu.VMEM((slots, PART_STEPS // LOADS, LANES, span_len), jnp.bfloat16),
            pltpu.VMEM((2, TAPS - 1, LANES, span_len), jnp.bfloat16),
            pltpu.VMEM((PART_STEPS + TAPS - 1, taps_rows, LANES), jnp.float32),
            pltpu.VMEM((rows * PART_STEPS, LANES), jnp.float32),
            pltpu.VMEM((pieces, rows // 2, depth, LANES), jnp.bfloat16),
            pltpu.VMEM((pieces, 2 * group, depth, LANES), jnp.bfloat16),
            pltpu.VMEM(piece, jnp.bfloat16),
            pltpu.VMEM(piece, jnp.bfloat16),
            pltpu.VMEM(piece, jnp.bfloat16),
            pltpu.VMEM(lhs, jnp.bfloat16),
            pltpu.SemaphoreType.DMA((slots,)),
            pltpu.SemaphoreType.DMA((2,)),
            pltpu.SemaphoreType.DMA((2, pieces)),
            pltpu.SemaphoreType.DMA((2, pieces)),
            pltpu.SemaphoreType.DMA((2, last - 1, pieces)),
            pltpu.SemaphoreType.DMA((2, last - 1, pieces)),
            pltpu.SemaphoreType.DMA((2, 2, pieces)),
            pltpu.SemaphoreType.DMA((2, 2, pieces)),
            pltpu.SemaphoreType.DMA((panel_len // LANES,)),
        ],
        compiler_params=pltpu.CompilerParams(
            collective_id=0, has_side_effects=True, vmem_limit_bytes=SPREAD_VMEM
        ),
    )(voltages)


def make_rhs(parts, panel, c):
    pieces = panel.shape[0]
    return jnp.concatenate(
        [
            jnp.concatenate([panel[q * parts + part, c] for part in range(parts)], axis=0)
            for q in range(pieces // parts)
        ],
        axis=1,
    )


def halves_rhs(parts, low, high, c):
    half = low.shape[1]
    return jnp.where(
        c < half, make_rhs(parts, low, jnp.minimum(c, half - 1)), make_rhs(parts, high, jnp.maximum(c - half, 0))
    )


def pair_tile(lhs_ref, c, rhs, tile):
    _, _, panel_len, depth = lhs_ref.shape
    steps = depth // 2
    sums = jnp.dot(lhs_ref[c].reshape(2 * panel_len, depth), rhs, preferred_element_type=jnp.float32)
    scaled = (sums * (1.0 / steps)).astype(jnp.bfloat16)
    tile[0] = scaled[:panel_len]
    tile[1] = scaled[panel_len:]


def tile_copy(tile, out_ref, c, panel, sem):
    panel_len = tile.shape[1]
    columns = pl.ds(pl.multiple_of(panel * panel_len, panel_len), panel_len)
    return pltpu.make_async_copy(tile, out_ref.at[c, :, :, columns], sem)


def near_kernel(n, parts, lhs_ref, own_ref, near_ref, low0, high0, low1, high1, out_ref, tiles, sems,
                own_sems):
    chans = lhs_ref.shape[0]
    place = place_of(lax.axis_index("blk"), n)
    last = n // 2 - 1
    makers = []
    for slot in range(near_ref.shape[0]):
        hop, side = slot // 2 + 1, slot % 2
        makers.append((place - hop * (1 - 2 * side), lambda c, slot=slot: make_rhs(parts, near_ref.at[slot], c)))
    makers.append((place - last, lambda c: halves_rhs(parts, low0, high0, c)))
    makers.append((place + last, lambda c: halves_rhs(parts, low1, high1, c)))

    def copy(c, i):
        return tile_copy(tiles.at[i], out_ref, c, block_at(makers[i][0], n), sems.at[i])

    def own_copy(c):
        return tile_copy(own_ref.at[c], out_ref, c, block_at(place, n), own_sems.at[c])

    for c in range(chans):
        own_copy(c).start()

    def one_channel(c, carry):
        for i, (_, rhs) in enumerate(makers):
            @pl.when(c > 0)
            def _():
                copy(c, i).wait()

            pair_tile(lhs_ref, c, rhs(c), tiles.at[i])
            copy(c, i).start()
        return carry

    lax.fori_loop(0, chans, one_channel, 0)
    for i in range(len(makers)):
        copy(0, i).wait()
    for c in range(chans):
        own_copy(c).wait()


def across_kernel(n, parts, lhs_ref, low, high, _, out_ref, tiles, sems):
    chans = lhs_ref.shape[0]
    panel = block_at(place_of(lax.axis_index("blk"), n) + n // 2, n)

    def copy(c):
        return tile_copy(tiles.at[c], out_ref, c, panel, sems.at[c])

    for c in range(chans):
        source, index = (low, c) if c < chans // 2 else (high, c - chans // 2)
        pair_tile(lhs_ref, c, make_rhs(parts, source, index), tiles.at[c])
        copy(c).start()
    for c in range(chans):
        copy(c).wait()


def correlate(kernel, count, parts, lhs, operands, visibilities=None):
    n = lax.axis_size("blk")
    chans, _, panel_len, depth = lhs.shape
    specs = [pl.BlockSpec(memory_space=pltpu.VMEM)] * (1 + len(operands))
    extra, aliases, buffers = [], {}, count
    if visibilities is not None:
        extra, aliases, buffers = [visibilities], {len(specs): 0}, chans
        specs = specs + [pl.BlockSpec(memory_space=pl.ANY)]
    tile_bytes = chans * count * 2 * panel_len * panel_len * 2
    return pl.pallas_call(
        functools.partial(kernel, n, parts),
        in_specs=specs,
        out_specs=pl.BlockSpec(memory_space=pl.ANY),
        out_shape=jax.ShapeDtypeStruct((chans, 2, panel_len, n * panel_len), jnp.bfloat16),
        input_output_aliases=aliases,
        scratch_shapes=[
            pltpu.VMEM((buffers, 2, panel_len, panel_len), jnp.bfloat16),
            pltpu.SemaphoreType.DMA((buffers,)),
        ]
        + [pltpu.SemaphoreType.DMA((chans,))] * (visibilities is None),
        cost_estimate=pl.CostEstimate(
            flops=tile_bytes * depth, bytes_accessed=tile_bytes * 5 // 4, transcendentals=0
        ),
        compiler_params=pltpu.CompilerParams(vmem_limit_bytes=PAIR_VMEM),
    )(lhs, *operands, *extra)


def body(voltages):
    n = lax.axis_size("blk")
    parts = (voltages.shape[0] - TAPS + 1) // PART_STEPS
    lhs, tiles, near, low0, high0, low1, high1 = spread(voltages)
    order = [2 * p if p < n // 2 else 2 * n - 1 - 2 * p for p in range(n)]
    low = lax.ppermute(low0, "blk", [(order[p], order[(p + 1) % n]) for p in range(n)])
    high = lax.ppermute(high1, "blk", [(order[p], order[(p - 1) % n]) for p in range(n)])
    visibilities = correlate(near_kernel, n - 2, parts, lhs, (tiles, near, low0, high0, low1, high1))
    return correlate(across_kernel, 1, parts, lhs, (low, high), visibilities)


def solution(mesh):
    return jax.shard_map(
        body,
        mesh=mesh,
        in_specs=(P(None, "blk", ("sec", "ch")),),
        out_specs=P(("sec", "ch"), None, "blk", None),
        check_vma=False,
    )
```
